32 devices in a mesh: az: 8 (over y, x, core), rg: 4 (over z).
Axes of the slice: x: 2, y: 2, z: 4, core: 2. Of those that a mesh axis runs over, the one named last changes fastest.
Arguments:
- reference_slc: bfloat16 [2, 768, 12288], P(None, 'az', 'rg'), may hold values from -6 to 6
- secondary_slc: bfloat16 [2, 768, 12288], P(None, 'az', 'rg'), may hold values from -6 to 6
- chip_offsets: int32 [2, 8, 384], P(None, 'az', 'rg'), may hold values from -80 to 80, as said below
- src_row: int32 [768], replicated, may hold values from 0 to 767, as said below
- line_owner: int32 [768], replicated, may hold values from 0 to 31, as said below
- band_start: int32 [12288], replicated, may hold values from -64 to 12343, as said below
- band_taps: bfloat16 [8, 12288], replicated, may hold values from -2.09375 to 2.09375
Outputs:
- est_offsets: float32 [2, 8, 384], P(None, 'az', 'rg')
- resampled: bfloat16 [2, 1024, 12288], P(None, ('az', 'rg'))
The draws below stay inside these ranges and needn't reach their ends.
Inputs may be any that keep to these rules, and one draw needn't show every extreme that they name: chip_offsets[0] lies within -80 and 80, chip_offsets[1] within -48 and 48. `src_row`: the source row of line i lies within 8 rows of i. `line_owner`: for every owner and every azimuth tile, at most 4 lines of that owner take their source rows from that tile, and an owner holds at most 32 lines; both bounds are met in every draw. band_start[j] lies within j - 64 and j + 56.
All inputs are finite; a program needn't handle non-finite values.
Results may differ from the reference program's by a relative error of at most 0.008.
Values may be sent and summed in bfloat16 or wider, within the bound.
A program may use at most 128 MiB of HBM per device.

```python
import math
import jax
import jax.numpy as jnp
from jax import lax

CHIP_LEN = 64
OVERSAMPLE = 16
LAG_COUNT = 48
TAP_COUNT = 8
SPACING = 32
MARGIN = 64
MAX_SHIFT = 8
LINES_DEV = 96
TILES_AZ = 8
ALL_LINES = 768
ALL_COLUMNS = 12288
CHIPS_ALL = 384
REF_RIM = 16
AZ_REACH = 80
RG_REACH = 48
OWNERS = 32
BUSY_OWNERS = 4
CALM_OWNERS = 28
PAIR_CAP = 4
OWNER_CAP = 32


def plan_lines(key):
    base = jax.random.fold_in(key, 71)
    shift_key = jax.random.fold_in(base, 1)
    order_key = jax.random.fold_in(base, 2)
    turn_key = jax.random.fold_in(base, 3)
    line_ids = jnp.arange(ALL_LINES, dtype=jnp.int32)
    line_moves = jax.random.randint(shift_key, (ALL_LINES,), -MAX_SHIFT, MAX_SHIFT + 1)
    line_moves = line_moves.at[0].set(-MAX_SHIFT).at[ALL_LINES - 1].set(MAX_SHIFT)
    source = jnp.clip(line_ids + line_moves, 0, ALL_LINES - 1)
    tile_of = source // LINES_DEV
    tile_hot = (tile_of[:, None] == jnp.arange(TILES_AZ, dtype=jnp.int32)[None, :]).astype(jnp.int32)
    tile_rank = jnp.sum(jnp.cumsum(tile_hot, axis=0) * tile_hot, axis=1) - 1
    shuffled = jax.random.permutation(order_key, OWNERS)
    heavy_set = shuffled[:BUSY_OWNERS]
    light_set = shuffled[BUSY_OWNERS:]
    light_turn = jax.random.randint(turn_key, (TILES_AZ,), 0, CALM_OWNERS)
    heavy_pick = heavy_set[jnp.minimum(tile_rank // PAIR_CAP, BUSY_OWNERS - 1)]
    light_pick = light_set[(tile_rank - PAIR_CAP * BUSY_OWNERS + light_turn[tile_of]) % CALM_OWNERS]
    owners = jnp.where(tile_rank < PAIR_CAP * BUSY_OWNERS, heavy_pick, light_pick)
    return (source.astype(jnp.int32), owners.astype(jnp.int32))


def draw_src_row(key, part):
    return plan_lines(key)[0]


def draw_line_owner(key, part):
    return plan_lines(key)[1]


def draw_chip_offsets(key, part):
    az_key = jax.random.fold_in(key, 5)
    rg_key = jax.random.fold_in(key, 6)
    az_part = jax.random.randint(az_key, (TILES_AZ, CHIPS_ALL), -AZ_REACH, AZ_REACH + 1)
    az_part = az_part.at[0, 0].set(-AZ_REACH).at[TILES_AZ - 1, CHIPS_ALL - 1].set(AZ_REACH)
    rg_part = jax.random.randint(rg_key, (TILES_AZ, CHIPS_ALL), -RG_REACH, RG_REACH + 1)
    rg_part = rg_part.at[0, 1].set(-RG_REACH).at[TILES_AZ - 1, 0].set(RG_REACH)
    return jnp.stack([az_part, rg_part]).astype(jnp.int32)


def draw_band_start(key, part):
    jitter = jax.random.randint(jax.random.fold_in(key, 9), (ALL_COLUMNS,), -MARGIN, MARGIN - TAP_COUNT + 1)
    jitter = jitter.at[0].set(-MARGIN).at[ALL_COLUMNS - 1].set(MARGIN - TAP_COUNT)
    return (jnp.arange(ALL_COLUMNS, dtype=jnp.int32) + jitter).astype(jnp.int32)


def levels(rng, shape, shards, smallest, top_value):
    def one(axis_at, parts):
        steps = jax.random.uniform(jax.random.fold_in(jax.random.fold_in(rng, 6), axis_at), (parts,), jnp.float32, smallest / len(shards), top_value / len(shards))
        return jnp.repeat(jnp.exp(steps), shape[axis_at] // parts).reshape((-1,) + (1,) * (len(shape) - axis_at - 1))

    gain = one(*shards[0])
    for cut in shards[1:]:
        gain = gain * one(*cut)
    return gain


def centred(own_key, shape, spread, bound, shards=(), held_as=jnp.bfloat16):
    result = spread * jax.random.normal(own_key, shape, jnp.float32)
    if shards:
        result = result * levels(own_key, shape, shards, -0.22, 0.18)
    return jnp.clip(result, -bound, bound).astype(held_as)


def setup_inputs(seed: int = 0) -> dict:
    arg_keys = jax.random.split(jax.random.key(seed), 8)
    return {
        "reference_slc": centred(arg_keys[0], (2, ALL_LINES, ALL_COLUMNS), 1.0, 6.0, ((1, 8), (2, 4))),
        "secondary_slc": centred(arg_keys[1], (2, ALL_LINES, ALL_COLUMNS), 1.0, 6.0, ((1, 8), (2, 4))),
        "chip_offsets": draw_chip_offsets(jax.random.fold_in(arg_keys[7], 71), 0),
        "src_row": draw_src_row(jax.random.fold_in(arg_keys[7], 71), 0),
        "line_owner": draw_line_owner(jax.random.fold_in(arg_keys[7], 71), 0),
        "band_start": draw_band_start(jax.random.fold_in(arg_keys[7], 71), 0),
        "band_taps": centred(arg_keys[6], (TAP_COUNT, ALL_COLUMNS), 0.35, 2.09375),
    }


PHASE_RATE = 2.0
EPS = 1e-06

def make_tables():
    indices = jnp.arange(CHIP_LEN, dtype=jnp.int32)
    product = indices[:, None] * indices[None, :] % CHIP_LEN
    angles = -2.0 * math.pi / CHIP_LEN * product.astype(jnp.float32)
    scaling = 1.0 / math.sqrt(CHIP_LEN)
    four_re = (jnp.cos(angles) * scaling).astype(jnp.bfloat16)
    four_im = (jnp.sin(angles) * scaling).astype(jnp.bfloat16)
    lag_steps = jnp.arange(LAG_COUNT, dtype=jnp.int32) - LAG_COUNT // 2
    frequency = jnp.where(indices < CHIP_LEN // 2, indices, indices - CHIP_LEN)
    phase_turns = lag_steps[:, None] * frequency[None, :] % (OVERSAMPLE * CHIP_LEN)
    lifted = 2.0 * math.pi / (OVERSAMPLE * CHIP_LEN) * phase_turns.astype(jnp.float32)
    lift_re = (jnp.cos(lifted) * scaling).astype(jnp.bfloat16)
    lift_im = (jnp.sin(lifted) * scaling).astype(jnp.bfloat16)
    lag_values = lag_steps.astype(jnp.float32) / OVERSAMPLE
    return (four_re, four_im, lift_re, lift_im, lag_values)

def rounded(values):
    return lax.optimization_barrier(values.astype(jnp.bfloat16)).astype(jnp.float32)

def spectrum(chip_re, chip_im, four_re, four_im):
    half_re = rounded(jnp.einsum('px,xgy->pgy', four_re, chip_re) - jnp.einsum('px,xgy->pgy', four_im, chip_im))
    half_im = rounded(jnp.einsum('px,xgy->pgy', four_re, chip_im) + jnp.einsum('px,xgy->pgy', four_im, chip_re))
    spec_re = jnp.einsum('pgy,qy->pgq', half_re, four_re) - jnp.einsum('pgy,qy->pgq', half_im, four_im)
    spec_im = jnp.einsum('pgy,qy->pgq', half_re, four_im) + jnp.einsum('pgy,qy->pgq', half_im, four_re)
    return (spec_re, spec_im)

def reference(reference_slc, secondary_slc, chip_offsets, src_row, line_owner, band_start, band_taps):
    four_re, four_im, lift_re, lift_im, lag_values = make_tables()
    four_re = four_re.astype(jnp.float32)
    four_im = four_im.astype(jnp.float32)
    lift_re = lift_re.astype(jnp.float32)
    lift_im = lift_im.astype(jnp.float32)
    sec_pad = jnp.pad(secondary_slc, ((0, 0), (MARGIN, MARGIN), (MARGIN, MARGIN)))
    first_row = LINES_DEV // 2 - CHIP_LEN // 2
    block_total = CHIPS_ALL + CHIP_LEN // SPACING - 1

    def per_tile(tile_index):
        row_first = (tile_index * LINES_DEV + first_row).astype(jnp.int32)
        ref_rows = lax.dynamic_slice(reference_slc, (jnp.int32(0), row_first, jnp.int32(0)), (2, CHIP_LEN, ALL_COLUMNS))
        offsets = lax.dynamic_index_in_dim(chip_offsets, tile_index, axis=1, keepdims=False)
        padded = jnp.pad(ref_rows, ((0, 0), (0, 0), (REF_RIM, REF_RIM)))
        blocks = padded.reshape(2, CHIP_LEN, block_total, SPACING)
        ref_chips = jnp.concatenate([blocks[:, :, start_block:start_block + CHIPS_ALL] for start_block in range(CHIP_LEN // SPACING)], axis=3)
        row_start = (row_first + offsets[0] + MARGIN).astype(jnp.int32)
        col_start = (SPACING * jnp.arange(CHIPS_ALL, dtype=jnp.int32) - REF_RIM + offsets[1] + MARGIN).astype(jnp.int32)

        def cut_chip(row_first_one, col_first_one):
            return lax.dynamic_slice(sec_pad, (jnp.int32(0), row_first_one, col_first_one), (2, CHIP_LEN, CHIP_LEN))
        sec_chips = jax.vmap(cut_chip)(row_start, col_start).transpose(1, 2, 0, 3)
        ref_re, ref_im = spectrum(ref_chips[0].astype(jnp.float32), ref_chips[1].astype(jnp.float32), four_re, four_im)
        sec_re, sec_im = spectrum(sec_chips[0].astype(jnp.float32), sec_chips[1].astype(jnp.float32), four_re, four_im)
        cross_re = rounded(ref_re * sec_re + ref_im * sec_im)
        cross_im = rounded(ref_im * sec_re - ref_re * sec_im)
        mid_re = rounded(jnp.einsum('pgq,vq->pgv', cross_re, lift_re) - jnp.einsum('pgq,vq->pgv', cross_im, lift_im))
        mid_im = rounded(jnp.einsum('pgq,vq->pgv', cross_re, lift_im) + jnp.einsum('pgq,vq->pgv', cross_im, lift_re))
        corr_re = jnp.einsum('up,pgv->ugv', lift_re, mid_re) - jnp.einsum('up,pgv->ugv', lift_im, mid_im)
        corr_im = jnp.einsum('up,pgv->ugv', lift_re, mid_im) + jnp.einsum('up,pgv->ugv', lift_im, mid_re)
        energy = corr_re * corr_re + corr_im * corr_im
        weight_map = energy * energy
        totals = lax.optimization_barrier(jnp.sum(weight_map, axis=(0, 2))) + EPS
        cent_az = jnp.einsum('u,ugv->g', lag_values, weight_map) / totals
        cent_rg = jnp.einsum('v,ugv->g', lag_values, weight_map) / totals
        return jnp.stack([offsets[0].astype(jnp.float32) + cent_az, offsets[1].astype(jnp.float32) + cent_rg])
    est_tiles = lax.map(per_tile, jnp.arange(TILES_AZ, dtype=jnp.int32))
    est_offsets = jnp.transpose(est_tiles, (1, 0, 2))
    line_data = jnp.take(secondary_slc, src_row, axis=1)
    padded_lines = jnp.pad(line_data, ((0, 0), (0, 0), (MARGIN, MARGIN)))
    summed = jnp.zeros((2, ALL_LINES, ALL_COLUMNS), jnp.float32)
    for tap_index in range(TAP_COUNT):
        picked = jnp.take(padded_lines, (band_start + tap_index + MARGIN).astype(jnp.int32), axis=2).astype(jnp.float32)
        summed = summed + picked * band_taps[tap_index].astype(jnp.float32)[None, None, :]
    field_rows = jnp.take(est_offsets[0], (src_row // LINES_DEV).astype(jnp.int32), axis=0)
    phase_angle = PHASE_RATE * jnp.repeat(field_rows, SPACING, axis=1)
    cosine = jnp.cos(phase_angle)
    sine_part = jnp.sin(phase_angle)
    line_re = summed[0] * cosine + summed[1] * sine_part
    line_im = summed[1] * cosine - summed[0] * sine_part
    lines_done = jnp.stack([line_re, line_im]).astype(jnp.bfloat16)
    line_ids = jnp.arange(ALL_LINES, dtype=jnp.int32)
    same_owner = line_owner[:, None] == line_owner[None, :]
    earlier = line_ids[:, None] > line_ids[None, :]
    own_rank = lax.optimization_barrier(jnp.sum((same_owner & earlier).astype(jnp.int32), axis=1))
    position = (line_owner * OWNER_CAP + own_rank).astype(jnp.int32)
    resampled = jnp.zeros((2, OWNERS * OWNER_CAP, ALL_COLUMNS), jnp.bfloat16).at[:, position, :].set(lines_done)
    return (est_offsets, resampled)
```

```python
import functools
import math

import jax
import jax.numpy as jnp
import numpy as np
from jax import lax
from jax.experimental import pallas as pl
from jax.experimental.pallas import tpu as pltpu
from jax.sharding import PartitionSpec as P

CHIP_LEN = 64
OVERSAMPLE = 16
LAG_COUNT = 48
TAP_COUNT = 8
SPACING = 32
MARGIN = 64
MAX_SHIFT = 8
LANES = 128
GROUP = 8

PHASE_RATE = 2.0
EPS = 1e-06
VMEM_LIMIT = 56 * 1024 * 1024


def make_tables():
    indices = np.arange(CHIP_LEN)
    product = indices[:, None] * indices[None, :] % CHIP_LEN
    angles = (-2.0 * math.pi / CHIP_LEN) * product
    scaling = 1.0 / math.sqrt(CHIP_LEN)
    four_re = np.cos(angles) * scaling
    four_im = np.sin(angles) * scaling
    lag_steps = np.arange(LAG_COUNT) - LAG_COUNT // 2
    frequency = np.where(indices < CHIP_LEN // 2, indices, indices - CHIP_LEN)
    phase_turns = lag_steps[:, None] * frequency[None, :] % (OVERSAMPLE * CHIP_LEN)
    lifted = 2.0 * math.pi / (OVERSAMPLE * CHIP_LEN) * phase_turns
    lift_re = np.cos(lifted) * scaling
    lift_im = np.sin(lifted) * scaling
    lag_values = (lag_steps / OVERSAMPLE).astype(np.float32)

    def left(re, im):
        return np.block([[re, -im], [im, re]])

    def right(re, im):
        pad = ((0, CHIP_LEN - re.shape[0]), (0, 0))
        re2 = np.kron(np.eye(2), np.pad(re, pad).T)
        im2 = np.kron(np.eye(2), np.pad(im, pad).T)
        return np.block([[re2, im2], [-im2, re2]])

    def held(table):
        return jnp.asarray(table.astype(np.float32)).astype(jnp.bfloat16)

    return (
        held(left(four_re, four_im)),
        held(right(four_re, four_im)),
        held(right(lift_re, lift_im)),
        held(left(lift_re, lift_im)),
        lag_values,
    )


def dot(a, b):
    return jnp.dot(a, b, preferred_element_type=jnp.float32)


ROWS = 16
CHUNK = 512


def place_bands(rel_ref, taps_ref, bands):
    place = lax.broadcasted_iota(jnp.int32, (2 * LANES, LANES), 0)

    def step(b, carry):
        cols = pl.ds(pl.multiple_of(b * LANES, LANES), LANES)
        delta = place - rel_ref[0:1, cols]
        taps = taps_ref[:, cols].astype(jnp.float32)
        band = jnp.zeros((2 * LANES, LANES), jnp.float32)
        for t in range(TAP_COUNT):
            band = jnp.where(delta == t, taps[t : t + 1], band)
        bands[b] = band.astype(jnp.bfloat16)
        return carry

    lax.fori_loop(0, bands.shape[0], step, 0)


def fill_windows(ref_ref, sec_ref, halos, ref_win, sec_win):
    top, low, left, right, ref_left, ref_right, top_left, top_right, low_left, low_right = halos
    lines = sec_ref.shape[1]
    blocks = sec_ref.shape[2] // LANES
    first = lines // 2 - CHIP_LEN // 2
    high = MARGIN + lines
    f32 = jnp.float32
    for c in range(2):
        for b in range(blocks):
            at = slice(b * LANES, (b + 1) * LANES)
            ref_win[c, b + 1] = ref_ref[c, first : first + CHIP_LEN, at].astype(f32)
            sec_win[c, b + 1, :MARGIN] = top[c, :, at].astype(f32)
            sec_win[c, b + 1, MARGIN:high] = sec_ref[c, :, at].astype(f32)
            sec_win[c, b + 1, high:] = low[c, :, at].astype(f32)
        ref_win[c, 0] = ref_left[c].astype(f32)
        ref_win[c, blocks + 1] = ref_right[c].astype(f32)
        for b, (above, beside, below) in (
            (0, (top_left, left, low_left)),
            (blocks + 1, (top_right, right, low_right)),
        ):
            sec_win[c, b, :MARGIN] = above[c].astype(f32)
            sec_win[c, b, MARGIN:high] = beside[c].astype(f32)
            sec_win[c, b, high:] = below[c].astype(f32)


def estimate(off_ref, tables, base_ref, ref_win, sec_win, plain_ref, lagged_ref, est_ref):
    four_ref, spec_ref, lift_ref, corr_ref, lag_ref, wide_ref = tables
    chips = off_ref.shape[1]
    lines = sec_win.shape[2] - 2 * MARGIN
    rim = (CHIP_LEN - SPACING) // 2
    first = lines // 2 - CHIP_LEN // 2
    lane = lax.broadcasted_iota(jnp.int32, (CHIP_LEN, LANES), 1)

    def placed(win, c, row, col, half):
        block = col // LANES
        inner = col - block * LANES
        near = win[c, block, pl.ds(row, CHIP_LEN), :]
        far = win[c, block + 1, pl.ds(row, CHIP_LEN), :]
        turn = (half * CHIP_LEN - inner + LANES) % LANES
        near = pltpu.roll(near, turn, 1)
        far = pltpu.roll(far, turn, 1)
        return jnp.where(lane - half * CHIP_LEN + inner < LANES, near, far)

    def pair(win, rows, cols_at):
        parts = []
        for c in range(2):
            even = placed(win, c, rows[0], cols_at[0], 0)
            odd = placed(win, c, rows[1], cols_at[1], 1)
            parts.append(jnp.where(lane < CHIP_LEN, even, odd).astype(jnp.bfloat16))
        return jnp.concatenate(parts, axis=0)

    def step(i, carry):
        ref_chips, sec_chips = [], []
        for j in range(GROUP):
            g = (i * GROUP + j) * 2
            at = [LANES + SPACING * (g + h) - rim for h in range(2)]
            ref_chips.append(pair(ref_win, (0, 0), at))
            rows = [MARGIN + first + off_ref[0, g + h] for h in range(2)]
            sec_chips.append(pair(sec_win, rows, [at[h] + off_ref[1, g + h] for h in range(2)]))
        both = jnp.concatenate(ref_chips + sec_chips, axis=1)
        half = dot(four_ref[...], both).astype(jnp.bfloat16)
        lhs = jnp.concatenate(
            [
                jnp.concatenate(
                    [
                        half[:CHIP_LEN, j * LANES : (j + 1) * LANES],
                        half[CHIP_LEN:, j * LANES : (j + 1) * LANES],
                    ],
                    axis=1,
                )
                for j in range(2 * GROUP)
            ],
            axis=0,
        )
        spec = dot(lhs, spec_ref[...])
        rows = GROUP * CHIP_LEN
        rr, ri = spec[:rows, :LANES], spec[:rows, LANES:]
        sr, si = spec[rows:, :LANES], spec[rows:, LANES:]
        cross = jnp.concatenate([rr * sr + ri * si, ri * sr - rr * si], axis=1)
        mid = dot(cross.astype(jnp.bfloat16), lift_ref[...]).astype(jnp.bfloat16)
        tall = jnp.concatenate(
            [
                jnp.concatenate(
                    [
                        mid[j * CHIP_LEN : (j + 1) * CHIP_LEN, :LANES],
                        mid[j * CHIP_LEN : (j + 1) * CHIP_LEN, LANES:],
                    ],
                    axis=0,
                )
                for j in range(GROUP)
            ],
            axis=1,
        )
        corr = dot(corr_ref[...], tall)
        energy = corr[:LAG_COUNT] * corr[:LAG_COUNT] + corr[LAG_COUNT:] * corr[LAG_COUNT:]
        weight = energy * energy
        plain = jnp.sum(weight, axis=0, keepdims=True)
        lagged = jnp.sum(weight * lag_ref[...], axis=0, keepdims=True)
        for j in range(GROUP):
            at = slice(j * LANES, (j + 1) * LANES)
            plain_ref[pl.ds(i * GROUP + j, 1), :] = plain[:, at]
            lagged_ref[pl.ds(i * GROUP + j, 1), :] = lagged[:, at]
        return carry

    lax.fori_loop(0, chips // (2 * GROUP), step, 0)
    near = lax.broadcasted_iota(jnp.int32, (chips // 2, LANES), 1) < CHIP_LEN
    plain = plain_ref[...]
    lagged = lagged_ref[...]
    across = plain * wide_ref[...]
    lane = lax.broadcasted_iota(jnp.int32, (chips // 2, LANES), 1)
    place = lax.broadcasted_iota(jnp.int32, (chips // 2, LANES), 0) * 2
    rows = [jnp.zeros((chips // 2, LANES), jnp.float32)] * 2
    for h in range(2):
        inside = near if h == 0 else jnp.logical_not(near)
        total = jnp.sum(jnp.where(inside, plain, 0.0), axis=1, keepdims=True) + EPS
        for c, moment in enumerate((lagged, across)):
            centre = jnp.sum(jnp.where(inside, moment, 0.0), axis=1, keepdims=True) / total
            rows[c] = jnp.where(lane == place + h, centre, rows[c])
    for c in range(2):
        est_ref[c : c + 1, :] = jnp.sum(rows[c], axis=0, keepdims=True) + base_ref[c : c + 1, :]


def fused_kernel(
    group_rows, far_first, off_ref, ref_ref, sec_ref, send_pick, recv_pick, rel_ref, taps_ref,
    tile_ref, four_ref, spec_ref, lift_ref, corr_ref, lag_ref, wide_ref, base_ref, est_ref,
    out_ref, outgoing, arrived, top, low, left, right, ref_left, ref_right, top_left, top_right,
    low_left, low_right, ref_win, sec_win, plain_ref, lagged_ref, bands, wide, mine, everyone,
    halo_send, halo_recv, bulk_send, bulk_recv, est_send, est_recv,
):
    az_count = lax.axis_size("az")
    rg_count = lax.axis_size("rg")
    az = lax.axis_index("az")
    rg = lax.axis_index("rg")
    me = az * rg_count + rg
    owners = az_count * rg_count
    lines = sec_ref.shape[1]
    cols = sec_ref.shape[2]
    groups = ROWS // group_rows
    part = cols // groups
    first = lines // 2 - CHIP_LEN // 2
    mesh_ids = pl.DeviceIdType.MESH

    def for_others(body):
        def plane(d, carry):
            def one(k, inner):
                body((az + k) % az_count, (rg + d) % rg_count)
                return inner

            return lax.fori_loop(jnp.where(d == 0, 1, 0), az_count, one, carry)

        lax.fori_loop(0, rg_count, plane, 0)

    barrier = pltpu.get_barrier_semaphore()

    def greet(a, r):
        pl.semaphore_signal(barrier, inc=1, device_id=(a, r), device_id_type=mesh_ids)

    for_others(greet)

    rows = jnp.concatenate([sec_ref[0], sec_ref[1]], axis=0)
    for at in range(0, part, CHUNK):
        width = min(CHUNK, part - at)
        picked = [
            dot(send_pick[g], rows[:, g * part + at : g * part + at + width])
            for g in range(send_pick.shape[0])
        ]
        if group_rows == 8:
            picked = [
                dot(send_pick[0], rows[:, g * part + at : g * part + at + width]).reshape(
                    owners, group_rows, width
                )
                for g in range(groups)
            ]
            tall = jnp.concatenate(picked, axis=1)
        else:
            tall = sum(picked).reshape(owners, ROWS, width)
        outgoing[:, :, at : at + width] = tall.astype(jnp.bfloat16)

    pl.semaphore_wait(barrier, owners - 1)

    high = lines - MARGIN
    last = cols - LANES
    middle = pl.ds(first, CHIP_LEN)
    moves = (
        (1, 0, sec_ref.at[:, pl.ds(high, MARGIN), :], top),
        (-1, 0, sec_ref.at[:, pl.ds(0, MARGIN), :], low),
        (0, 1, sec_ref.at[:, :, pl.ds(last, LANES)], left),
        (0, -1, sec_ref.at[:, :, pl.ds(0, LANES)], right),
        (0, 1, ref_ref.at[:, middle, pl.ds(last, LANES)], ref_left),
        (0, -1, ref_ref.at[:, middle, pl.ds(0, LANES)], ref_right),
        (1, 1, sec_ref.at[:, pl.ds(high, MARGIN), pl.ds(last, LANES)], top_left),
        (1, -1, sec_ref.at[:, pl.ds(high, MARGIN), pl.ds(0, LANES)], top_right),
        (-1, 1, sec_ref.at[:, pl.ds(0, MARGIN), pl.ds(last, LANES)], low_left),
        (-1, -1, sec_ref.at[:, pl.ds(0, MARGIN), pl.ds(0, LANES)], low_right),
    )

    def inside(a, r):
        return (a >= 0) & (a < az_count) & (r >= 0) & (r < rg_count)

    def halo(which):
        step_a, step_r, source, target = moves[which]
        return pltpu.make_async_remote_copy(
            src_ref=source,
            dst_ref=target,
            send_sem=halo_send.at[which],
            recv_sem=halo_recv.at[which],
            device_id=(
                (az + step_a + az_count) % az_count,
                (rg + step_r + rg_count) % rg_count,
            ),
            device_id_type=mesh_ids,
        )

    for which, (step_a, step_r, _, target) in enumerate(moves):
        @pl.when(inside(az + step_a, rg + step_r))
        def _():
            halo(which).start()

        @pl.when(jnp.logical_not(inside(az - step_a, rg - step_r)))
        def _():
            target[...] = jnp.zeros_like(target)

    def bulk(d):
        to = (rg + d) % rg_count

        def one(k, carry):
            a = (az + k) % az_count
            pltpu.make_async_remote_copy(
                src_ref=outgoing.at[a * rg_count + to],
                dst_ref=arrived.at[rg, az],
                send_sem=bulk_send,
                recv_sem=bulk_recv.at[d],
                device_id=(a, to),
                device_id_type=mesh_ids,
            ).start()
            return carry

        lax.fori_loop(1 if d == 0 else 0, az_count, one, 0)

    for d in far_first:
        bulk(d)
    arrived[rg, az] = outgoing[az * rg_count + rg]

    place_bands(rel_ref, taps_ref, bands)

    for which, (step_a, step_r, _, _) in enumerate(moves):
        @pl.when(inside(az - step_a, rg - step_r))
        def _():
            halo(which).wait_recv()

    halos = (
        top, low, left, right, ref_left, ref_right, top_left, top_right, low_left, low_right
    )
    fill_windows(ref_ref, sec_ref, halos, ref_win, sec_win)
    tables = (four_ref, spec_ref, lift_ref, corr_ref, lag_ref, wide_ref)
    estimate(off_ref, tables, base_ref, ref_win, sec_win, plain_ref, lagged_ref, est_ref)
    mine[...] = est_ref[0:1, :]
    everyone[me] = est_ref[0:1, :]

    def tell(a, r):
        pltpu.make_async_remote_copy(
            src_ref=mine,
            dst_ref=everyone.at[me],
            send_sem=est_send,
            recv_sem=est_recv,
            device_id=(a, r),
            device_id_type=mesh_ids,
        ).start()

    for_others(tell)

    owned = out_ref.shape[1]
    per_plane = cols // LANES
    wide[0, :, :MARGIN] = jnp.zeros((2 * owned, MARGIN), jnp.bfloat16)
    wide[rg_count - 1, :, MARGIN + cols :] = jnp.zeros((2 * owned, MARGIN), jnp.bfloat16)
    told = everyone.at[pl.ds(0, owners - 1)]
    pltpu.make_async_copy(told, told, est_recv).wait()

    lane = lax.broadcasted_iota(jnp.int32, (owned, LANES), 1) // SPACING
    tile = tile_ref[...]

    def turns(plane):
        angle = jnp.zeros((owned, LANES), jnp.float32)
        for a in range(az_count):
            angle = jnp.where(tile == a, everyone[a * rg_count + plane], angle)
        angle = PHASE_RATE * angle
        return jnp.cos(angle), jnp.sin(angle)

    def finish(plane, k, cosine, sine):
        b = plane * per_plane + k
        cols_at = pl.ds(pl.multiple_of(b * LANES, LANES), LANES)
        window = wide[plane, :, pl.ds(pl.multiple_of(k * LANES, LANES), 2 * LANES)]
        s = dot(window, bands[b])
        chip = lane + k * (LANES // SPACING)
        cos_k = jnp.take_along_axis(cosine, chip, axis=1)
        sin_k = jnp.take_along_axis(sine, chip, axis=1)
        s_re = s[:owned]
        s_im = s[owned:]
        out_ref[0, :, cols_at] = (s_re * cos_k + s_im * sin_k).astype(jnp.bfloat16)
        out_ref[1, :, cols_at] = (s_im * cos_k - s_re * sin_k).astype(jnp.bfloat16)

    for d in far_first:
        plane = (rg + rg_count - d) % rg_count
        landed = arrived.at[plane]
        if d == 0:
            landed = landed.at[pl.ds(0, az_count - 1)]
        pltpu.make_async_copy(landed, landed, bulk_recv.at[d]).wait()
        held = arrived[plane].reshape(az_count * ROWS, part)
        for g in range(groups):
            at = MARGIN + g * part
            wide[plane, :, at : at + part] = dot(recv_pick[g], held).astype(jnp.bfloat16)

        @pl.when(plane > 0)
        def _():
            wide[plane - 1, :, MARGIN + cols :] = wide[plane, :, MARGIN : 2 * MARGIN]

        @pl.when(plane < rg_count - 1)
        def _():
            wide[plane + 1, :, :MARGIN] = wide[plane, :, cols : MARGIN + cols]

        cosine, sine = turns(plane)
        inner = per_plane - 2
        unroll = next(u for u in (11, 10, 8, 7, 6, 5, 4, 3, 2, 1) if inner % u == 0)

        def some(i, carry):
            for j in range(unroll):
                finish(plane, 1 + i * unroll + j, cosine, sine)
            return carry

        lax.fori_loop(0, inner // unroll, some, 0)

    def edges(plane, carry):
        cosine, sine = turns(plane)
        finish(plane, 0, cosine, sine)
        finish(plane, per_plane - 1, cosine, sine)
        return carry

    lax.fori_loop(0, rg_count, edges, 0)

    for which, (step_a, step_r, _, _) in enumerate(moves):
        @pl.when(inside(az + step_a, rg + step_r))
        def _():
            halo(which).wait_send()

    gone = outgoing.at[pl.ds(0, owners - 1)]
    pltpu.make_async_copy(gone, gone, bulk_send).wait()
    pltpu.make_async_copy(told, told, est_send).wait()


def fused(offsets, ref, sec, send_pick, recv_pick, rel, taps, tile, tables, az_count, rg_count,
          owner_cap, group_rows):
    four, spec, lift, corr, lags = tables
    lines = sec.shape[1]
    cols = sec.shape[2]
    chips = cols // SPACING
    blocks = cols // LANES
    owners = az_count * rg_count
    part = cols * group_rows // ROWS
    far_first = sorted(range(1, rg_count), key=lambda d: abs(d - rg_count // 2)) + [0]
    vmem = pl.BlockSpec(memory_space=pltpu.VMEM)
    lag_wide = np.tile(np.pad(lags, (0, CHIP_LEN - LAG_COUNT)), 2)[None, :]
    bf16 = jnp.bfloat16
    f32 = jnp.float32
    args = (
        offsets, ref, sec, send_pick, recv_pick, rel, taps, tile, four, spec, lift, corr,
        jnp.asarray(lags)[:, None], jnp.asarray(lag_wide),
        jnp.pad(offsets, ((0, 0), (0, LANES - chips))).astype(f32),
    )
    return pl.pallas_call(
        functools.partial(fused_kernel, group_rows, tuple(far_first)),
        in_specs=[pl.BlockSpec(memory_space=pltpu.SMEM)] + [vmem] * (len(args) - 1),
        out_specs=(vmem, vmem),
        out_shape=(
            jax.ShapeDtypeStruct((2, LANES), f32),
            jax.ShapeDtypeStruct((2, owner_cap, cols * rg_count), bf16),
        ),
        scratch_shapes=[
            pltpu.VMEM((owners, ROWS, part), bf16),
            pltpu.VMEM((rg_count, az_count, ROWS, part), bf16),
            pltpu.VMEM((2, MARGIN, cols), bf16),
            pltpu.VMEM((2, MARGIN, cols), bf16),
            pltpu.VMEM((2, lines, LANES), bf16),
            pltpu.VMEM((2, lines, LANES), bf16),
            pltpu.VMEM((2, CHIP_LEN, LANES), bf16),
            pltpu.VMEM((2, CHIP_LEN, LANES), bf16),
            pltpu.VMEM((2, MARGIN, LANES), bf16),
            pltpu.VMEM((2, MARGIN, LANES), bf16),
            pltpu.VMEM((2, MARGIN, LANES), bf16),
            pltpu.VMEM((2, MARGIN, LANES), bf16),
            pltpu.VMEM((2, blocks + 3, CHIP_LEN, LANES), f32),
            pltpu.VMEM((2, blocks + 3, lines + 2 * MARGIN, LANES), f32),
            pltpu.VMEM((chips // 2, LANES), f32),
            pltpu.VMEM((chips // 2, LANES), f32),
            pltpu.VMEM((cols * rg_count // LANES, 2 * LANES, LANES), bf16),
            pltpu.VMEM((rg_count, 2 * owner_cap, cols + 2 * MARGIN), bf16),
            pltpu.VMEM((1, LANES), f32),
            pltpu.VMEM((owners, 1, LANES), f32),
            pltpu.SemaphoreType.DMA((10,)),
            pltpu.SemaphoreType.DMA((10,)),
            pltpu.SemaphoreType.DMA,
            pltpu.SemaphoreType.DMA((rg_count,)),
            pltpu.SemaphoreType.DMA,
            pltpu.SemaphoreType.DMA,
        ],
        compiler_params=pltpu.CompilerParams(
            vmem_limit_bytes=VMEM_LIMIT, collective_id=0, has_side_effects=True
        ),
        name="fused",
    )(*args)


def per_device(
    reference_slc, secondary_slc, chip_offsets, src_row, line_owner, band_start, band_taps
):
    tables = make_tables()
    lines_dev = secondary_slc.shape[1]
    cols_dev = secondary_slc.shape[2]
    chip_count = cols_dev // SPACING
    az_count = lax.axis_size("az")
    rg_count = lax.axis_size("rg")
    owners = az_count * rg_count
    pair_cap = max(2, (lines_dev + 2 * MAX_SHIFT + owners - 1) // owners)
    owner_cap = pair_cap * az_count
    group_rows = 2 * pair_cap
    groups = ROWS // group_rows
    total_cols = cols_dev * rg_count
    az_index = lax.axis_index("az")
    rg_index = lax.axis_index("rg")
    me_owner = az_index * rg_count + rg_index

    count = src_row.shape[0]
    ids = jnp.arange(count, dtype=jnp.int32)
    src_tile = src_row // lines_dev
    mine = (line_owner[:, None] == line_owner[None, :]) & (ids[:, None] < ids[None, :])
    own_rank = jnp.sum(mine.astype(jnp.int32), axis=0)
    near = mine & (src_tile[:, None] == src_tile[None, :])
    pair_rank = jnp.sum(near.astype(jnp.int32), axis=0)

    local_row = src_row - az_index * lines_dev
    slot = jnp.where(src_tile == az_index, line_owner * pair_cap + pair_rank, -1)
    slots = jnp.arange(owners * pair_cap, dtype=jnp.int32)
    send_row = jnp.sum(
        jnp.where(slots[:, None] == slot[None, :], local_row[None, :] + 1, 0), axis=1
    ) - 1
    send_row = send_row.reshape(owners, 1, pair_cap)
    part = jnp.arange(2, dtype=jnp.int32)[None, :, None] * lines_dev
    target = jnp.where(send_row >= 0, send_row + part, -1).reshape(owners, 1, group_rows)
    if group_rows == 8:
        target = target.reshape(1, owners * group_rows)
    else:
        group = jnp.arange(groups, dtype=jnp.int32)
        at_group = group[:, None, None, None] == group[None, None, :, None]
        target = jnp.where(at_group, target[None], -1).reshape(groups, owners * ROWS)
    send_pick = (
        target[:, :, None] == jnp.arange(2 * lines_dev, dtype=jnp.int32)[None, None, :]
    ).astype(jnp.bfloat16)

    all_cols = jnp.arange(total_cols, dtype=jnp.int32)
    rel = (band_start - all_cols // LANES * LANES + MARGIN)[None, :]

    outs = jnp.arange(owner_cap, dtype=jnp.int32)
    placed = (own_rank[None, :] == outs[:, None]) & (line_owner == me_owner)[None, :]
    which = jnp.sum(
        jnp.where(placed, (src_tile * pair_cap + pair_rank + 1)[None, :], 0), axis=1
    ) - 1
    tile = which // pair_cap
    from_rank = which % pair_cap
    group = jnp.arange(groups, dtype=jnp.int32)[:, None, None]
    parts = jnp.arange(2, dtype=jnp.int32)[None, :, None]
    source = (tile * ROWS + from_rank)[None, None] + group * group_rows + parts * pair_cap
    source = jnp.where(which[None, None] >= 0, source, -1).reshape(groups, 2 * owner_cap)
    recv_pick = (
        source[:, :, None] == jnp.arange(az_count * ROWS, dtype=jnp.int32)[None, None, :]
    ).astype(jnp.bfloat16)
    tile_wide = jnp.broadcast_to(tile[:, None], (owner_cap, LANES))

    est, lines_out = fused(
        chip_offsets[:, 0], reference_slc, secondary_slc, send_pick, recv_pick, rel, band_taps,
        tile_wide, tables, az_count, rg_count, owner_cap, group_rows,
    )
    return (est[:, None, :chip_count], lines_out)


def solution(mesh):
    return jax.shard_map(
        per_device,
        mesh=mesh,
        in_specs=(
            P(None, "az", "rg"),
            P(None, "az", "rg"),
            P(None, "az", "rg"),
            P(),
            P(),
            P(),
            P(),
        ),
        out_specs=(P(None, "az", "rg"), P(None, ("az", "rg"), None)),
        check_vma=False,
    )
```

```python
import functools
import math

import jax
import jax.numpy as jnp
import numpy as np
from jax import lax
from jax.experimental import pallas as pl
from jax.experimental.pallas import tpu as pltpu
from jax.sharding import PartitionSpec as P

CHIP_LEN = 64
OVERSAMPLE = 16
LAG_COUNT = 48
TAP_COUNT = 8
SPACING = 32
MARGIN = 64
MAX_SHIFT = 8
LANES = 128
GROUP = 8

PHASE_RATE = 2.0
EPS = 1e-06
VMEM_LIMIT = 56 * 1024 * 1024


def make_tables():
    indices = np.arange(CHIP_LEN)
    product = indices[:, None] * indices[None, :] % CHIP_LEN
    angles = (-2.0 * math.pi / CHIP_LEN) * product
    scaling = 1.0 / math.sqrt(CHIP_LEN)
    four_re = np.cos(angles) * scaling
    four_im = np.sin(angles) * scaling
    lag_steps = np.arange(LAG_COUNT) - LAG_COUNT // 2
    frequency = np.where(indices < CHIP_LEN // 2, indices, indices - CHIP_LEN)
    phase_turns = lag_steps[:, None] * frequency[None, :] % (OVERSAMPLE * CHIP_LEN)
    lifted = 2.0 * math.pi / (OVERSAMPLE * CHIP_LEN) * phase_turns
    lift_re = np.cos(lifted) * scaling
    lift_im = np.sin(lifted) * scaling
    lag_values = (lag_steps / OVERSAMPLE).astype(np.float32)

    def left(re, im):
        return np.block([[re, -im], [im, re]])

    def right(re, im):
        pad = ((0, CHIP_LEN - re.shape[0]), (0, 0))
        re2 = np.kron(np.eye(2), np.pad(re, pad).T)
        im2 = np.kron(np.eye(2), np.pad(im, pad).T)
        return np.block([[re2, im2], [-im2, re2]])

    def held(table):
        return jnp.asarray(table.astype(np.float32)).astype(jnp.bfloat16)

    return (
        held(left(four_re, four_im)),
        held(right(four_re, four_im)),
        held(right(lift_re, lift_im)),
        held(left(lift_re, lift_im)),
        lag_values,
    )


def dot(a, b):
    return jnp.dot(a, b, preferred_element_type=jnp.float32)


ROWS = 16
CHUNK = 512


def place_bands(start_ref, taps_ref, bands):
    place = lax.broadcasted_iota(jnp.int32, (2 * LANES, LANES), 0)

    def step(b, carry):
        cols = pl.ds(pl.multiple_of(b * LANES, LANES), LANES)
        delta = place - (start_ref[0:1, cols] - b * LANES + MARGIN)
        taps = taps_ref[:, cols].astype(jnp.float32)
        band = jnp.zeros((2 * LANES, LANES), jnp.float32)
        for t in range(TAP_COUNT):
            band = jnp.where(delta == t, taps[t : t + 1], band)
        bands[b] = band.astype(jnp.bfloat16)
        return carry

    lax.fori_loop(0, bands.shape[0], step, 0)


def plan_lines(src_ref, owner_ref, pair_cap, az, me, az_count, lines, recv_pick, tile_ref):
    f32 = jnp.float32
    count = src_ref.shape[1]
    owned = tile_ref.shape[0]
    owners = az_count * lax.axis_size("rg")
    group_rows = 2 * pair_cap
    groups = recv_pick.shape[0]
    src = src_ref[...].astype(f32)
    owner = owner_ref[...].astype(f32)
    tile = jnp.zeros_like(src)
    for a in range(1, az_count):
        tile = tile + jnp.where(src >= a * lines, 1.0, 0.0)
    az_f = az.astype(f32)
    owner_is_me = owner == me.astype(f32)

    def down(height, width):
        return lax.broadcasted_iota(jnp.int32, (height, width), 0).astype(f32)

    sent = jnp.where((down(owners, count) == owner) & (tile == az_f), 1.0, 0.0)
    got = jnp.where((down(az_count, count) == tile) & owner_is_me, 1.0, 0.0)
    own = jnp.broadcast_to(jnp.where(owner_is_me, 1.0, 0.0), (8, count))
    hot = jnp.concatenate([sent, got, own], axis=0).astype(jnp.bfloat16)
    ranks = []
    for at in range(0, count, 2 * LANES):
        before = lax.broadcasted_iota(jnp.int32, (count, 2 * LANES), 0)
        after = lax.broadcasted_iota(jnp.int32, (count, 2 * LANES), 1) + at
        earlier = jnp.where(before < after, 1.0, 0.0).astype(jnp.bfloat16)
        ranks.append(dot(hot, earlier))
    ranks = jnp.concatenate(ranks, axis=1)
    sent_rank = jnp.sum(sent * ranks[:owners], axis=0, keepdims=True)
    got_rank = jnp.sum(got * ranks[owners : owners + az_count], axis=0, keepdims=True)
    own_rank = ranks[owners + az_count : owners + az_count + 1]

    height = owners * (group_rows if group_rows == 8 else ROWS)
    row = lax.broadcasted_iota(jnp.int32, (height, LANES), 0)
    key = (row // (height // owners) * pair_cap + row % pair_cap).astype(f32)
    slot = jnp.where(tile == az_f, owner * pair_cap + sent_rank, -1.0)
    local = src - az_f * lines + 1.0
    found = jnp.zeros((height, LANES), f32)
    for at in range(0, count, LANES):
        cols = slice(at, at + LANES)
        found = found + jnp.where(slot[:, cols] == key, local[:, cols], 0.0)
    found = jnp.sum(found, axis=1, keepdims=True)
    row = lax.broadcasted_iota(jnp.int32, (height, 1), 0)
    half = (row // pair_cap % 2).astype(f32)
    target = jnp.where(found > 0.0, found - 1.0 + half * lines, -1.0)
    across = lax.broadcasted_iota(jnp.int32, (height, 2 * lines), 1).astype(f32)
    hit = jnp.where(across == target, 1.0, 0.0)
    if group_rows == 8:
        picks = [hit.astype(jnp.bfloat16)]
    else:
        group = row % ROWS // group_rows
        picks = [jnp.where(group == g, hit, 0.0).astype(jnp.bfloat16) for g in range(groups)]

    place = down(owned, LANES)
    code = jnp.where(owner_is_me, tile * ROWS + got_rank + 1.0, 0.0)
    found = jnp.zeros((owned, LANES), f32)
    for at in range(0, count, LANES):
        cols = slice(at, at + LANES)
        found = found + jnp.where(own_rank[:, cols] == place, code[:, cols], 0.0)
    found = jnp.sum(found, axis=1, keepdims=True)
    from_tile = jnp.where(found > 0.0, 0.0, -1.0)
    for a in range(1, az_count):
        from_tile = from_tile + jnp.where(found > a * ROWS, 1.0, 0.0)
    tile_ref[...] = jnp.broadcast_to(from_tile, tile_ref.shape)
    across = lax.broadcasted_iota(jnp.int32, (owned, az_count * ROWS), 1).astype(f32)
    for g in range(groups):
        for p in range(2):
            source = found - 1.0 + (g * group_rows + p * pair_cap)
            source = jnp.where(found > 0.0, source, -1.0)
            chosen = jnp.where(across == source, 1.0, 0.0).astype(jnp.bfloat16)
            recv_pick[g, p * owned : (p + 1) * owned, :] = chosen
    return picks


def fill_windows(ref_ref, sec_ref, halos, ref_win, sec_win):
    top, low, left, right, ref_left, ref_right, top_left, top_right, low_left, low_right = halos
    lines = sec_ref.shape[1]
    blocks = sec_ref.shape[2] // LANES
    first = lines // 2 - CHIP_LEN // 2
    high = MARGIN + lines
    f32 = jnp.float32
    for c in range(2):
        for b in range(blocks):
            at = slice(b * LANES, (b + 1) * LANES)
            ref_win[c, b + 1] = ref_ref[c, first : first + CHIP_LEN, at].astype(f32)
            sec_win[c, b + 1, :MARGIN] = top[c, :, at].astype(f32)
            sec_win[c, b + 1, MARGIN:high] = sec_ref[c, :, at].astype(f32)
            sec_win[c, b + 1, high:] = low[c, :, at].astype(f32)
        ref_win[c, 0] = ref_left[c].astype(f32)
        ref_win[c, blocks + 1] = ref_right[c].astype(f32)
        for b, (above, beside, below) in (
            (0, (top_left, left, low_left)),
            (blocks + 1, (top_right, right, low_right)),
        ):
            sec_win[c, b, :MARGIN] = above[c].astype(f32)
            sec_win[c, b, MARGIN:high] = beside[c].astype(f32)
            sec_win[c, b, high:] = below[c].astype(f32)


def estimate(off_ref, tables, base_ref, ref_win, sec_win, plain_ref, lagged_ref, est_ref, mine):
    four_ref, spec_ref, lift_ref, corr_ref, lag_ref, wide_ref = tables
    chips = off_ref.shape[2]
    lines = sec_win.shape[2] - 2 * MARGIN
    rim = (CHIP_LEN - SPACING) // 2
    first = lines // 2 - CHIP_LEN // 2
    lane = lax.broadcasted_iota(jnp.int32, (CHIP_LEN, LANES), 1)

    def placed(win, c, row, col, half):
        block = col // LANES
        inner = col - block * LANES
        near = win[c, block, pl.ds(row, CHIP_LEN), :]
        far = win[c, block + 1, pl.ds(row, CHIP_LEN), :]
        turn = (half * CHIP_LEN - inner + LANES) % LANES
        near = pltpu.roll(near, turn, 1)
        far = pltpu.roll(far, turn, 1)
        return jnp.where(lane - half * CHIP_LEN + inner < LANES, near, far)

    def pair(win, rows, cols_at):
        parts = []
        for c in range(2):
            even = placed(win, c, rows[0], cols_at[0], 0)
            odd = placed(win, c, rows[1], cols_at[1], 1)
            parts.append(jnp.where(lane < CHIP_LEN, even, odd).astype(jnp.bfloat16))
        return jnp.concatenate(parts, axis=0)

    def step(i, carry):
        ref_chips, sec_chips = [], []
        for j in range(GROUP):
            g = (i * GROUP + j) * 2
            at = [LANES + SPACING * (g + h) - rim for h in range(2)]
            ref_chips.append(pair(ref_win, (0, 0), at))
            rows = [MARGIN + first + off_ref[0, 0, g + h] for h in range(2)]
            sec_chips.append(pair(sec_win, rows, [at[h] + off_ref[1, 0, g + h] for h in range(2)]))
        both = jnp.concatenate(ref_chips + sec_chips, axis=1)
        half = dot(four_ref[...], both).astype(jnp.bfloat16)
        lhs = jnp.concatenate(
            [
                jnp.concatenate(
                    [
                        half[:CHIP_LEN, j * LANES : (j + 1) * LANES],
                        half[CHIP_LEN:, j * LANES : (j + 1) * LANES],
                    ],
                    axis=1,
                )
                for j in range(2 * GROUP)
            ],
            axis=0,
        )
        spec = dot(lhs, spec_ref[...])
        rows = GROUP * CHIP_LEN
        rr, ri = spec[:rows, :LANES], spec[:rows, LANES:]
        sr, si = spec[rows:, :LANES], spec[rows:, LANES:]
        cross = jnp.concatenate([rr * sr + ri * si, ri * sr - rr * si], axis=1)
        mid = dot(cross.astype(jnp.bfloat16), lift_ref[...]).astype(jnp.bfloat16)
        tall = jnp.concatenate(
            [
                jnp.concatenate(
                    [
                        mid[j * CHIP_LEN : (j + 1) * CHIP_LEN, :LANES],
                        mid[j * CHIP_LEN : (j + 1) * CHIP_LEN, LANES:],
                    ],
                    axis=0,
                )
                for j in range(GROUP)
            ],
            axis=1,
        )
        corr = dot(corr_ref[...], tall)
        energy = corr[:LAG_COUNT] * corr[:LAG_COUNT] + corr[LAG_COUNT:] * corr[LAG_COUNT:]
        weight = energy * energy
        plain = jnp.sum(weight, axis=0, keepdims=True)
        lagged = jnp.sum(weight * lag_ref[...], axis=0, keepdims=True)
        for j in range(GROUP):
            at = slice(j * LANES, (j + 1) * LANES)
            plain_ref[pl.ds(i * GROUP + j, 1), :] = plain[:, at]
            lagged_ref[pl.ds(i * GROUP + j, 1), :] = lagged[:, at]
        return carry

    lax.fori_loop(0, chips // (2 * GROUP), step, 0)
    near = lax.broadcasted_iota(jnp.int32, (chips // 2, LANES), 1) < CHIP_LEN
    plain = plain_ref[...]
    lagged = lagged_ref[...]
    across = plain * wide_ref[...]
    lane = lax.broadcasted_iota(jnp.int32, (chips // 2, LANES), 1)
    place = lax.broadcasted_iota(jnp.int32, (chips // 2, LANES), 0) * 2
    rows = [jnp.zeros((chips // 2, LANES), jnp.float32)] * 2
    for h in range(2):
        inside = near if h == 0 else jnp.logical_not(near)
        total = jnp.sum(jnp.where(inside, plain, 0.0), axis=1, keepdims=True) + EPS
        for c, moment in enumerate((lagged, across)):
            centre = jnp.sum(jnp.where(inside, moment, 0.0), axis=1, keepdims=True) / total
            rows[c] = jnp.where(lane == place + h, centre, rows[c])
    mine[...] = jnp.zeros_like(mine)
    for c in range(2):
        found = jnp.sum(rows[c], axis=0, keepdims=True)[:, :chips]
        est_ref[c] = found + base_ref[c].astype(jnp.float32)
    mine[:, :chips] = est_ref[0]


def fused_kernel(
    pair_cap, far_first, off_ref, base_ref, ref_ref, sec_ref, src_ref, owner_ref, start_ref,
    taps_ref, four_ref, spec_ref, lift_ref, corr_ref, lag_ref, wide_ref, est_ref, out_ref,
    recv_pick, tile_ref, outgoing, arrived, top, low, left, right, ref_left, ref_right, top_left,
    top_right, low_left, low_right, ref_win, sec_win, plain_ref, lagged_ref, bands, wide, mine,
    everyone, halo_send, halo_recv, bulk_send, bulk_recv, est_send, est_recv,
):
    group_rows = 2 * pair_cap
    az_count = lax.axis_size("az")
    rg_count = lax.axis_size("rg")
    az = lax.axis_index("az")
    rg = lax.axis_index("rg")
    me = az * rg_count + rg
    owners = az_count * rg_count
    lines = sec_ref.shape[1]
    cols = sec_ref.shape[2]
    groups = ROWS // group_rows
    part = cols // groups
    first = lines // 2 - CHIP_LEN // 2
    mesh_ids = pl.DeviceIdType.MESH

    def for_others(body):
        def plane(d, carry):
            def one(k, inner):
                body((az + k) % az_count, (rg + d) % rg_count)
                return inner

            return lax.fori_loop(jnp.where(d == 0, 1, 0), az_count, one, carry)

        lax.fori_loop(0, rg_count, plane, 0)

    barrier = pltpu.get_barrier_semaphore()

    def greet(a, r):
        pl.semaphore_signal(barrier, inc=1, device_id=(a, r), device_id_type=mesh_ids)

    for_others(greet)

    send_pick = plan_lines(
        src_ref, owner_ref, pair_cap, az, me, az_count, lines, recv_pick, tile_ref
    )
    rows = jnp.concatenate([sec_ref[0], sec_ref[1]], axis=0)
    for at in range(0, part, CHUNK):
        width = min(CHUNK, part - at)
        picked = [
            dot(send_pick[g % len(send_pick)], rows[:, g * part + at : g * part + at + width])
            for g in range(groups)
        ]
        if group_rows == 8:
            picked = [lines_g.reshape(owners, group_rows, width) for lines_g in picked]
            tall = jnp.concatenate(picked, axis=1)
        else:
            tall = sum(picked).reshape(owners, ROWS, width)
        outgoing[:, :, at : at + width] = tall.astype(jnp.bfloat16)

    pl.semaphore_wait(barrier, owners - 1)

    high = lines - MARGIN
    last = cols - LANES
    middle = pl.ds(first, CHIP_LEN)
    moves = (
        (1, 0, sec_ref.at[:, pl.ds(high, MARGIN), :], top),
        (-1, 0, sec_ref.at[:, pl.ds(0, MARGIN), :], low),
        (0, 1, sec_ref.at[:, :, pl.ds(last, LANES)], left),
        (0, -1, sec_ref.at[:, :, pl.ds(0, LANES)], right),
        (0, 1, ref_ref.at[:, middle, pl.ds(last, LANES)], ref_left),
        (0, -1, ref_ref.at[:, middle, pl.ds(0, LANES)], ref_right),
        (1, 1, sec_ref.at[:, pl.ds(high, MARGIN), pl.ds(last, LANES)], top_left),
        (1, -1, sec_ref.at[:, pl.ds(high, MARGIN), pl.ds(0, LANES)], top_right),
        (-1, 1, sec_ref.at[:, pl.ds(0, MARGIN), pl.ds(last, LANES)], low_left),
        (-1, -1, sec_ref.at[:, pl.ds(0, MARGIN), pl.ds(0, LANES)], low_right),
    )

    def inside(a, r):
        return (a >= 0) & (a < az_count) & (r >= 0) & (r < rg_count)

    def halo(which):
        step_a, step_r, source, target = moves[which]
        return pltpu.make_async_remote_copy(
            src_ref=source,
            dst_ref=target,
            send_sem=halo_send.at[which],
            recv_sem=halo_recv.at[which],
            device_id=(
                (az + step_a + az_count) % az_count,
                (rg + step_r + rg_count) % rg_count,
            ),
            device_id_type=mesh_ids,
        )

    for which, (step_a, step_r, _, target) in enumerate(moves):
        @pl.when(inside(az + step_a, rg + step_r))
        def _():
            halo(which).start()

        @pl.when(jnp.logical_not(inside(az - step_a, rg - step_r)))
        def _():
            target[...] = jnp.zeros_like(target)

    def partner(k):
        quads = az_count // 4
        turn_y = (az // 4 + k // 2) % quads
        turn_x = (az // 2 + k // (2 * quads)) % 2
        return (turn_y * 2 + turn_x) * 2 + (az + k) % 2

    def bulk(d, low_k, high_k):
        to = (rg + d) % rg_count

        def one(k, carry):
            a = partner(k)
            pltpu.make_async_remote_copy(
                src_ref=outgoing.at[a * rg_count + to],
                dst_ref=arrived.at[rg, az],
                send_sem=bulk_send,
                recv_sem=bulk_recv.at[d],
                device_id=(a, to),
                device_id_type=mesh_ids,
            ).start()
            return carry

        lax.fori_loop(low_k, high_k, one, 0)

    for low_k, high_k in ((0, az_count // 2), (az_count // 2, az_count)):
        for d in far_first:
            bulk(d, 1 if d == 0 and low_k == 0 else low_k, high_k)
    arrived[rg, az] = outgoing[az * rg_count + rg]

    place_bands(start_ref, taps_ref, bands)

    for which, (step_a, step_r, _, _) in enumerate(moves):
        @pl.when(inside(az - step_a, rg - step_r))
        def _():
            halo(which).wait_recv()

    halos = (
        top, low, left, right, ref_left, ref_right, top_left, top_right, low_left, low_right
    )
    fill_windows(ref_ref, sec_ref, halos, ref_win, sec_win)
    tables = (four_ref, spec_ref, lift_ref, corr_ref, lag_ref, wide_ref)
    estimate(
        off_ref, tables, base_ref, ref_win, sec_win, plain_ref, lagged_ref, est_ref, mine
    )
    everyone[me] = mine[...]

    def tell(a, r):
        pltpu.make_async_remote_copy(
            src_ref=mine,
            dst_ref=everyone.at[me],
            send_sem=est_send,
            recv_sem=est_recv,
            device_id=(a, r),
            device_id_type=mesh_ids,
        ).start()

    for_others(tell)

    owned = out_ref.shape[1]
    per_plane = cols // LANES
    wide[0, :, :MARGIN] = jnp.zeros((2 * owned, MARGIN), jnp.bfloat16)
    wide[rg_count - 1, :, MARGIN + cols :] = jnp.zeros((2 * owned, MARGIN), jnp.bfloat16)
    told = everyone.at[pl.ds(0, owners - 1)]
    pltpu.make_async_copy(told, told, est_recv).wait()

    lane = lax.broadcasted_iota(jnp.int32, (owned, LANES), 1) // SPACING
    tile = tile_ref[...]

    def turns(plane):
        angle = jnp.zeros((owned, LANES), jnp.float32)
        for a in range(az_count):
            angle = jnp.where(tile == a, everyone[a * rg_count + plane], angle)
        angle = PHASE_RATE * angle
        return jnp.cos(angle), jnp.sin(angle)

    def finish(plane, k, cosine, sine):
        b = plane * per_plane + k
        cols_at = pl.ds(pl.multiple_of(b * LANES, LANES), LANES)
        window = wide[plane, :, pl.ds(pl.multiple_of(k * LANES, LANES), 2 * LANES)]
        s = dot(window, bands[b])
        chip = lane + k * (LANES // SPACING)
        cos_k = jnp.take_along_axis(cosine, chip, axis=1)
        sin_k = jnp.take_along_axis(sine, chip, axis=1)
        s_re = s[:owned]
        s_im = s[owned:]
        out_ref[0, :, cols_at] = (s_re * cos_k + s_im * sin_k).astype(jnp.bfloat16)
        out_ref[1, :, cols_at] = (s_im * cos_k - s_re * sin_k).astype(jnp.bfloat16)

    for d in far_first:
        plane = (rg + rg_count - d) % rg_count
        landed = arrived.at[plane]
        if d == 0:
            landed = landed.at[pl.ds(0, az_count - 1)]
        pltpu.make_async_copy(landed, landed, bulk_recv.at[d]).wait()
        held = arrived[plane].reshape(az_count * ROWS, part)
        for g in range(groups):
            at = MARGIN + g * part
            wide[plane, :, at : at + part] = dot(recv_pick[g], held).astype(jnp.bfloat16)

        @pl.when(plane > 0)
        def _():
            wide[plane - 1, :, MARGIN + cols :] = wide[plane, :, MARGIN : 2 * MARGIN]

        @pl.when(plane < rg_count - 1)
        def _():
            wide[plane + 1, :, :MARGIN] = wide[plane, :, cols : MARGIN + cols]

        cosine, sine = turns(plane)
        inner = per_plane - 2
        unroll = next(u for u in (11, 10, 8, 7, 6, 5, 4, 3, 2, 1) if inner % u == 0)

        def some(i, carry):
            for j in range(unroll):
                finish(plane, 1 + i * unroll + j, cosine, sine)
            return carry

        lax.fori_loop(0, inner // unroll, some, 0)

    def edges(plane, carry):
        cosine, sine = turns(plane)
        finish(plane, 0, cosine, sine)
        finish(plane, per_plane - 1, cosine, sine)
        return carry

    lax.fori_loop(0, rg_count, edges, 0)

    for which, (step_a, step_r, _, _) in enumerate(moves):
        @pl.when(inside(az + step_a, rg + step_r))
        def _():
            halo(which).wait_send()

    gone = outgoing.at[pl.ds(0, owners - 1)]
    pltpu.make_async_copy(gone, gone, bulk_send).wait()
    pltpu.make_async_copy(told, told, est_send).wait()


def fused(offsets, ref, sec, src_row, line_owner, band_start, taps, tables, az_count, rg_count):
    four, spec, lift, corr, lags = tables
    lines = sec.shape[1]
    cols = sec.shape[2]
    chips = cols // SPACING
    blocks = cols // LANES
    owners = az_count * rg_count
    pair_cap = max(2, (lines + 2 * MAX_SHIFT + owners - 1) // owners)
    owner_cap = pair_cap * az_count
    groups = ROWS // (2 * pair_cap)
    part = cols // groups
    far_first = sorted(range(1, rg_count), key=lambda d: abs(d - rg_count // 2)) + [0]
    vmem = pl.BlockSpec(memory_space=pltpu.VMEM)
    lag_wide = np.tile(np.pad(lags, (0, CHIP_LEN - LAG_COUNT)), 2)[None, :]
    bf16 = jnp.bfloat16
    f32 = jnp.float32
    args = (
        offsets, offsets, ref, sec, src_row[None], line_owner[None], band_start[None], taps,
        four, spec, lift, corr, jnp.asarray(lags)[:, None], jnp.asarray(lag_wide),
    )
    return pl.pallas_call(
        functools.partial(fused_kernel, pair_cap, tuple(far_first)),
        in_specs=[pl.BlockSpec(memory_space=pltpu.SMEM)] + [vmem] * (len(args) - 1),
        out_specs=(vmem, vmem),
        out_shape=(
            jax.ShapeDtypeStruct((2, 1, chips), f32),
            jax.ShapeDtypeStruct((2, owner_cap, cols * rg_count), bf16),
        ),
        scratch_shapes=[
            pltpu.VMEM((groups, 2 * owner_cap, az_count * ROWS), bf16),
            pltpu.VMEM((owner_cap, LANES), f32),
            pltpu.VMEM((owners, ROWS, part), bf16),
            pltpu.VMEM((rg_count, az_count, ROWS, part), bf16),
            pltpu.VMEM((2, MARGIN, cols), bf16),
            pltpu.VMEM((2, MARGIN, cols), bf16),
            pltpu.VMEM((2, lines, LANES), bf16),
            pltpu.VMEM((2, lines, LANES), bf16),
            pltpu.VMEM((2, CHIP_LEN, LANES), bf16),
            pltpu.VMEM((2, CHIP_LEN, LANES), bf16),
            pltpu.VMEM((2, MARGIN, LANES), bf16),
            pltpu.VMEM((2, MARGIN, LANES), bf16),
            pltpu.VMEM((2, MARGIN, LANES), bf16),
            pltpu.VMEM((2, MARGIN, LANES), bf16),
            pltpu.VMEM((2, blocks + 3, CHIP_LEN, LANES), f32),
            pltpu.VMEM((2, blocks + 3, lines + 2 * MARGIN, LANES), f32),
            pltpu.VMEM((chips // 2, LANES), f32),
            pltpu.VMEM((chips // 2, LANES), f32),
            pltpu.VMEM((cols * rg_count // LANES, 2 * LANES, LANES), bf16),
            pltpu.VMEM((rg_count, 2 * owner_cap, cols + 2 * MARGIN), bf16),
            pltpu.VMEM((1, LANES), f32),
            pltpu.VMEM((owners, 1, LANES), f32),
            pltpu.SemaphoreType.DMA((10,)),
            pltpu.SemaphoreType.DMA((10,)),
            pltpu.SemaphoreType.DMA,
            pltpu.SemaphoreType.DMA((rg_count,)),
            pltpu.SemaphoreType.DMA,
            pltpu.SemaphoreType.DMA,
        ],
        compiler_params=pltpu.CompilerParams(
            vmem_limit_bytes=VMEM_LIMIT, collective_id=0, has_side_effects=True
        ),
        name="fused",
    )(*args)


def per_device(
    reference_slc, secondary_slc, chip_offsets, src_row, line_owner, band_start, band_taps
):
    return fused(
        chip_offsets, reference_slc, secondary_slc, src_row, line_owner, band_start, band_taps,
        make_tables(), lax.axis_size("az"), lax.axis_size("rg"),
    )


def solution(mesh):
    return jax.shard_map(
        per_device,
        mesh=mesh,
        in_specs=(
            P(None, "az", "rg"),
            P(None, "az", "rg"),
            P(None, "az", "rg"),
            P(),
            P(),
            P(),
            P(),
        ),
        out_specs=(P(None, "az", "rg"), P(None, ("az", "rg"), None)),
        check_vma=False,
    )
```

```python
import functools
import math

import jax
import jax.numpy as jnp
import numpy as np
from jax import lax
from jax.experimental import pallas as pl
from jax.experimental.pallas import tpu as pltpu
from jax.sharding import PartitionSpec as P

CHIP_LEN = 64
OVERSAMPLE = 16
LAG_COUNT = 48
TAP_COUNT = 8
SPACING = 32
MARGIN = 64
MAX_SHIFT = 8
LANES = 128
GROUP = 8

PHASE_RATE = 2.0
EPS = 1e-06
VMEM_LIMIT = 62 * 1024 * 1024


def make_tables():
    indices = np.arange(CHIP_LEN)
    product = indices[:, None] * indices[None, :] % CHIP_LEN
    angles = (-2.0 * math.pi / CHIP_LEN) * product
    scaling = 1.0 / math.sqrt(CHIP_LEN)
    four_re = np.cos(angles) * scaling
    four_im = np.sin(angles) * scaling
    lag_steps = np.arange(LAG_COUNT) - LAG_COUNT // 2
    frequency = np.where(indices < CHIP_LEN // 2, indices, indices - CHIP_LEN)
    phase_turns = lag_steps[:, None] * frequency[None, :] % (OVERSAMPLE * CHIP_LEN)
    lifted = 2.0 * math.pi / (OVERSAMPLE * CHIP_LEN) * phase_turns
    lift_re = np.cos(lifted) * scaling
    lift_im = np.sin(lifted) * scaling
    lag_values = (lag_steps / OVERSAMPLE).astype(np.float32)

    def left(re, im):
        return np.block([[re, -im], [im, re]])

    def right(re, im):
        pad = ((0, CHIP_LEN - re.shape[0]), (0, 0))
        re2 = np.kron(np.eye(2), np.pad(re, pad).T)
        im2 = np.kron(np.eye(2), np.pad(im, pad).T)
        return np.block([[re2, im2], [-im2, re2]])

    def held(table):
        return jnp.asarray(table.astype(np.float32)).astype(jnp.bfloat16)

    return (
        held(left(four_re, four_im)),
        held(right(four_re, four_im)),
        held(right(lift_re, lift_im)),
        held(left(lift_re, lift_im)),
        lag_values,
    )


def dot(a, b):
    return jnp.dot(a, b, preferred_element_type=jnp.float32)


ROWS = 16
HOLD = 4
CHUNK = 512


def place_bands(start_ref, taps_ref, bands):
    place = lax.broadcasted_iota(jnp.int32, (2 * LANES, LANES), 0)

    def step(b, carry):
        cols = pl.ds(pl.multiple_of(b * LANES, LANES), LANES)
        delta = place - (start_ref[0:1, cols] - b * LANES + MARGIN)
        taps = taps_ref[:, cols].astype(jnp.float32)
        band = jnp.zeros((2 * LANES, LANES), jnp.float32)
        for t in range(TAP_COUNT):
            band = jnp.where(delta == t, taps[t : t + 1], band)
        bands[b] = band.astype(jnp.bfloat16)
        return carry

    lax.fori_loop(0, bands.shape[0], step, 0)


def plan_lines(src_ref, owner_ref, pair_cap, az, me, az_count, lines, recv_pick, tile_ref):
    f32 = jnp.float32
    count = src_ref.shape[0]
    owned = tile_ref.shape[0]
    owners = az_count * lax.axis_size("rg")
    group_rows = 2 * pair_cap
    groups = recv_pick.shape[0]
    src = src_ref[...].reshape(1, count).astype(f32)
    owner = owner_ref[...].reshape(1, count).astype(f32)
    tile = jnp.zeros_like(src)
    for a in range(1, az_count):
        tile = tile + jnp.where(src >= a * lines, 1.0, 0.0)
    az_f = az.astype(f32)
    owner_is_me = owner == me.astype(f32)

    def down(height, width):
        return lax.broadcasted_iota(jnp.int32, (height, width), 0).astype(f32)

    sent = jnp.where((down(owners, count) == owner) & (tile == az_f), 1.0, 0.0)
    got = jnp.where((down(az_count, count) == tile) & owner_is_me, 1.0, 0.0)
    own = jnp.broadcast_to(jnp.where(owner_is_me, 1.0, 0.0), (8, count))
    hot = jnp.concatenate([sent, got, own], axis=0).astype(jnp.bfloat16)
    ranks = []
    for at in range(0, count, 2 * LANES):
        before = lax.broadcasted_iota(jnp.int32, (count, 2 * LANES), 0)
        after = lax.broadcasted_iota(jnp.int32, (count, 2 * LANES), 1) + at
        earlier = jnp.where(before < after, 1.0, 0.0).astype(jnp.bfloat16)
        ranks.append(dot(hot, earlier))
    ranks = jnp.concatenate(ranks, axis=1)
    sent_rank = jnp.sum(sent * ranks[:owners], axis=0, keepdims=True)
    got_rank = jnp.sum(got * ranks[owners : owners + az_count], axis=0, keepdims=True)
    own_rank = ranks[owners + az_count : owners + az_count + 1]

    height = owners * (group_rows if group_rows == 8 else ROWS)
    row = lax.broadcasted_iota(jnp.int32, (height, LANES), 0)
    key = (row // (height // owners) * pair_cap + row % pair_cap).astype(f32)
    slot = jnp.where(tile == az_f, owner * pair_cap + sent_rank, -1.0)
    local = src - az_f * lines + 1.0
    found = jnp.zeros((height, LANES), f32)
    for at in range(0, count, LANES):
        cols = slice(at, at + LANES)
        found = found + jnp.where(slot[:, cols] == key, local[:, cols], 0.0)
    found = jnp.sum(found, axis=1, keepdims=True)
    row = lax.broadcasted_iota(jnp.int32, (height, 1), 0)
    half = (row // pair_cap % 2).astype(f32)
    target = jnp.where(found > 0.0, found - 1.0 + half * lines, -1.0)
    across = lax.broadcasted_iota(jnp.int32, (height, 2 * lines), 1).astype(f32)
    hit = jnp.where(across == target, 1.0, 0.0)
    if group_rows == 8:
        picks = [hit.astype(jnp.bfloat16)]
    else:
        group = row % ROWS // group_rows
        picks = [jnp.where(group == g, hit, 0.0).astype(jnp.bfloat16) for g in range(groups)]

    place = down(owned, LANES)
    code = jnp.where(owner_is_me, tile * ROWS + got_rank + 1.0, 0.0)
    found = jnp.zeros((owned, LANES), f32)
    for at in range(0, count, LANES):
        cols = slice(at, at + LANES)
        found = found + jnp.where(own_rank[:, cols] == place, code[:, cols], 0.0)
    found = jnp.sum(found, axis=1, keepdims=True)
    from_tile = jnp.where(found > 0.0, 0.0, -1.0)
    for a in range(1, az_count):
        from_tile = from_tile + jnp.where(found > a * ROWS, 1.0, 0.0)
    tile_ref[...] = jnp.broadcast_to(from_tile, tile_ref.shape)
    across = lax.broadcasted_iota(jnp.int32, (owned, az_count * ROWS), 1).astype(f32)
    for g in range(groups):
        for p in range(2):
            source = found - 1.0 + (g * group_rows + p * pair_cap)
            source = jnp.where(found > 0.0, source, -1.0)
            chosen = jnp.where(across == source, 1.0, 0.0).astype(jnp.bfloat16)
            recv_pick[g, p * owned : (p + 1) * owned, :] = chosen
    return picks


def fill_windows(ref_ref, sec_ref, halos, ref_win, sec_win):
    top, low, left, right, ref_left, ref_right, top_left, top_right, low_left, low_right = halos
    lines = sec_ref.shape[1]
    blocks = sec_ref.shape[2] // LANES
    first = lines // 2 - CHIP_LEN // 2
    high = MARGIN + lines
    f32 = jnp.float32
    for c in range(2):
        for b in range(blocks):
            at = slice(b * LANES, (b + 1) * LANES)
            ref_win[c, b + 1] = ref_ref[c, first : first + CHIP_LEN, at].astype(f32)
            sec_win[c, b + 1, :MARGIN] = top[c, :, at].astype(f32)
            sec_win[c, b + 1, MARGIN:high] = sec_ref[c, :, at].astype(f32)
            sec_win[c, b + 1, high:] = low[c, :, at].astype(f32)
        ref_win[c, 0] = ref_left[c].astype(f32)
        ref_win[c, blocks + 1] = ref_right[c].astype(f32)
        for b, (above, beside, below) in (
            (0, (top_left, left, low_left)),
            (blocks + 1, (top_right, right, low_right)),
        ):
            sec_win[c, b, :MARGIN] = above[c].astype(f32)
            sec_win[c, b, MARGIN:high] = beside[c].astype(f32)
            sec_win[c, b, high:] = below[c].astype(f32)


def estimate(off_ref, tables, base_ref, ref_win, sec_win, plain_ref, lagged_ref, est_ref, mine):
    four_ref, spec_ref, lift_ref, corr_ref, lag_ref, wide_ref = tables
    chips = off_ref.shape[2]
    lines = sec_win.shape[2] - 2 * MARGIN
    rim = (CHIP_LEN - SPACING) // 2
    first = lines // 2 - CHIP_LEN // 2
    lane = lax.broadcasted_iota(jnp.int32, (CHIP_LEN, LANES), 1)

    def placed(win, c, row, col, half):
        block = col // LANES
        inner = col - block * LANES
        near = win[c, block, pl.ds(row, CHIP_LEN), :]
        far = win[c, block + 1, pl.ds(row, CHIP_LEN), :]
        turn = (half * CHIP_LEN - inner + LANES) % LANES
        near = pltpu.roll(near, turn, 1)
        far = pltpu.roll(far, turn, 1)
        return jnp.where(lane - half * CHIP_LEN + inner < LANES, near, far)

    def pair(win, rows, cols_at):
        parts = []
        for c in range(2):
            even = placed(win, c, rows[0], cols_at[0], 0)
            odd = placed(win, c, rows[1], cols_at[1], 1)
            parts.append(jnp.where(lane < CHIP_LEN, even, odd).astype(jnp.bfloat16))
        return jnp.concatenate(parts, axis=0)

    def step(i, carry):
        ref_chips, sec_chips = [], []
        for j in range(GROUP):
            g = (i * GROUP + j) * 2
            at = [LANES + SPACING * (g + h) - rim for h in range(2)]
            ref_chips.append(pair(ref_win, (0, 0), at))
            rows = [MARGIN + first + off_ref[0, 0, g + h] for h in range(2)]
            sec_chips.append(pair(sec_win, rows, [at[h] + off_ref[1, 0, g + h] for h in range(2)]))
        both = jnp.concatenate(ref_chips + sec_chips, axis=1)
        half = dot(four_ref[...], both).astype(jnp.bfloat16)
        lhs = jnp.concatenate(
            [
                jnp.concatenate(
                    [
                        half[:CHIP_LEN, j * LANES : (j + 1) * LANES],
                        half[CHIP_LEN:, j * LANES : (j + 1) * LANES],
                    ],
                    axis=1,
                )
                for j in range(2 * GROUP)
            ],
            axis=0,
        )
        spec = dot(lhs, spec_ref[...])
        rows = GROUP * CHIP_LEN
        rr, ri = spec[:rows, :LANES], spec[:rows, LANES:]
        sr, si = spec[rows:, :LANES], spec[rows:, LANES:]
        cross = jnp.concatenate([rr * sr + ri * si, ri * sr - rr * si], axis=1)
        mid = dot(cross.astype(jnp.bfloat16), lift_ref[...]).astype(jnp.bfloat16)
        tall = jnp.concatenate(
            [
                jnp.concatenate(
                    [
                        mid[j * CHIP_LEN : (j + 1) * CHIP_LEN, :LANES],
                        mid[j * CHIP_LEN : (j + 1) * CHIP_LEN, LANES:],
                    ],
                    axis=0,
                )
                for j in range(GROUP)
            ],
            axis=1,
        )
        corr = dot(corr_ref[...], tall)
        energy = corr[:LAG_COUNT] * corr[:LAG_COUNT] + corr[LAG_COUNT:] * corr[LAG_COUNT:]
        weight = energy * energy
        plain = jnp.sum(weight, axis=0, keepdims=True)
        lagged = jnp.sum(weight * lag_ref[...], axis=0, keepdims=True)
        for j in range(GROUP):
            at = slice(j * LANES, (j + 1) * LANES)
            plain_ref[pl.ds(i * GROUP + j, 1), :] = plain[:, at]
            lagged_ref[pl.ds(i * GROUP + j, 1), :] = lagged[:, at]
        return carry

    lax.fori_loop(0, chips // (2 * GROUP), step, 0)
    near = lax.broadcasted_iota(jnp.int32, (chips // 2, LANES), 1) < CHIP_LEN
    plain = plain_ref[...]
    lagged = lagged_ref[...]
    across = plain * wide_ref[...]
    lane = lax.broadcasted_iota(jnp.int32, (chips // 2, LANES), 1)
    place = lax.broadcasted_iota(jnp.int32, (chips // 2, LANES), 0) * 2
    rows = [jnp.zeros((chips // 2, LANES), jnp.float32)] * 2
    for h in range(2):
        inside = near if h == 0 else jnp.logical_not(near)
        total = jnp.sum(jnp.where(inside, plain, 0.0), axis=1, keepdims=True) + EPS
        for c, moment in enumerate((lagged, across)):
            centre = jnp.sum(jnp.where(inside, moment, 0.0), axis=1, keepdims=True) / total
            rows[c] = jnp.where(lane == place + h, centre, rows[c])
    mine[...] = jnp.zeros_like(mine)
    for c in range(2):
        est_ref[c] = jnp.sum(rows[c], axis=0, keepdims=True)[:, :chips]
    mine[:, :chips] = est_ref[0] + base_ref[0].astype(jnp.float32)


def fused_kernel(
    pair_cap, far_first, off_ref, src_hbm, owner_hbm, sec_hbm, ref_hbm, start_hbm, taps_hbm,
    four_hbm, spec_hbm, lift_hbm, corr_hbm, lag_hbm, wide_hbm, base_hbm, est_ref, out_ref,
    src_ref, owner_ref, sec_ref, ref_ref, start_ref, taps_ref, four_ref, spec_ref, lift_ref,
    corr_ref, lag_ref, wide_ref, base_ref, recv_pick, tile_ref, outgoing, arrived, top, low, left,
    right, ref_left, ref_right, top_left, top_right, low_left, low_right, ref_win, sec_win,
    plain_ref, lagged_ref, bands, wide, mine, everyone, load_sem, halo_send, halo_recv, bulk_send,
    bulk_recv, est_send, est_recv,
):
    loads = [
        pltpu.make_async_copy(source, target, load_sem.at[which])
        for which, (source, target) in enumerate((
            (src_hbm, src_ref), (owner_hbm, owner_ref), (sec_hbm, sec_ref), (ref_hbm, ref_ref),
            (start_hbm, start_ref), (taps_hbm, taps_ref), (four_hbm, four_ref),
            (spec_hbm, spec_ref), (lift_hbm, lift_ref), (corr_hbm, corr_ref),
            (lag_hbm, lag_ref), (wide_hbm, wide_ref), (base_hbm, base_ref),
        ))
    ]
    for load in loads:
        load.start()

    group_rows = 2 * pair_cap
    az_count = lax.axis_size("az")
    rg_count = lax.axis_size("rg")
    az = lax.axis_index("az")
    rg = lax.axis_index("rg")
    me = az * rg_count + rg
    owners = az_count * rg_count
    lines = sec_ref.shape[1]
    cols = sec_ref.shape[2]
    groups = ROWS // group_rows
    part = cols // groups
    first = lines // 2 - CHIP_LEN // 2
    mesh_ids = pl.DeviceIdType.MESH

    def for_others(body):
        def plane(d, carry):
            def one(k, inner):
                body((az + k) % az_count, (rg + d) % rg_count)
                return inner

            return lax.fori_loop(jnp.where(d == 0, 1, 0), az_count, one, carry)

        lax.fori_loop(0, rg_count, plane, 0)

    barrier = pltpu.get_barrier_semaphore()

    def greet(a, r):
        pl.semaphore_signal(barrier, inc=1, device_id=(a, r), device_id_type=mesh_ids)

    for_others(greet)

    loads[0].wait()
    loads[1].wait()
    send_pick = plan_lines(
        src_ref, owner_ref, pair_cap, az, me, az_count, lines, recv_pick, tile_ref
    )
    loads[2].wait()
    rows = jnp.concatenate([sec_ref[0], sec_ref[1]], axis=0)
    for at in range(0, part, CHUNK):
        width = min(CHUNK, part - at)
        picked = [
            dot(send_pick[g % len(send_pick)], rows[:, g * part + at : g * part + at + width])
            for g in range(groups)
        ]
        if group_rows == 8:
            picked = [lines_g.reshape(owners, group_rows, width) for lines_g in picked]
            tall = jnp.concatenate(picked, axis=1)
        else:
            tall = sum(picked).reshape(owners, ROWS, width)
        outgoing[:, :, at : at + width] = tall.astype(jnp.bfloat16)

    loads[3].wait()
    pl.semaphore_wait(barrier, owners - 1)

    high = lines - MARGIN
    last = cols - LANES
    middle = pl.ds(first, CHIP_LEN)
    moves = (
        (1, 0, sec_ref.at[:, pl.ds(high, MARGIN), :], top),
        (-1, 0, sec_ref.at[:, pl.ds(0, MARGIN), :], low),
        (0, 1, sec_ref.at[:, :, pl.ds(last, LANES)], left),
        (0, -1, sec_ref.at[:, :, pl.ds(0, LANES)], right),
        (0, 1, ref_ref.at[:, middle, pl.ds(last, LANES)], ref_left),
        (0, -1, ref_ref.at[:, middle, pl.ds(0, LANES)], ref_right),
        (1, 1, sec_ref.at[:, pl.ds(high, MARGIN), pl.ds(last, LANES)], top_left),
        (1, -1, sec_ref.at[:, pl.ds(high, MARGIN), pl.ds(0, LANES)], top_right),
        (-1, 1, sec_ref.at[:, pl.ds(0, MARGIN), pl.ds(last, LANES)], low_left),
        (-1, -1, sec_ref.at[:, pl.ds(0, MARGIN), pl.ds(0, LANES)], low_right),
    )

    def inside(a, r):
        return (a >= 0) & (a < az_count) & (r >= 0) & (r < rg_count)

    def halo(which):
        step_a, step_r, source, target = moves[which]
        return pltpu.make_async_remote_copy(
            src_ref=source,
            dst_ref=target,
            send_sem=halo_send.at[which],
            recv_sem=halo_recv.at[which],
            device_id=(
                (az + step_a + az_count) % az_count,
                (rg + step_r + rg_count) % rg_count,
            ),
            device_id_type=mesh_ids,
        )

    for which, (step_a, step_r, _, target) in enumerate(moves):
        @pl.when(inside(az + step_a, rg + step_r))
        def _():
            halo(which).start()

        @pl.when(jnp.logical_not(inside(az - step_a, rg - step_r)))
        def _():
            target[...] = jnp.zeros_like(target)

    def partner(k):
        quads = az_count // 4
        turn_y = (az // 4 + k // 2) % quads
        turn_x = (az // 2 + k // (2 * quads)) % 2
        return (turn_y * 2 + turn_x) * 2 + (az + k) % 2

    def bulk(d, low_k, high_k):
        to = (rg + d) % rg_count

        def one(k, carry):
            a = partner(k)
            pltpu.make_async_remote_copy(
                src_ref=outgoing.at[a * rg_count + to],
                dst_ref=arrived.at[rg, az],
                send_sem=bulk_send,
                recv_sem=bulk_recv.at[d],
                device_id=(a, to),
                device_id_type=mesh_ids,
            ).start()
            return carry

        lax.fori_loop(low_k, high_k, one, 0)

    half = az_count // 2
    groups_out = [(d, 1 if d == 0 else 0, half) for d in far_first]
    groups_out += [(d, half, az_count) for d in far_first]
    later = len(groups_out) - HOLD
    for group in groups_out[:later]:
        bulk(*group)
    arrived[rg, az] = outgoing[az * rg_count + rg]

    for load in loads[4:]:
        load.wait()
    place_bands(start_ref, taps_ref, bands)

    for which, (step_a, step_r, _, _) in enumerate(moves):
        @pl.when(inside(az - step_a, rg - step_r))
        def _():
            halo(which).wait_recv()

    halos = (
        top, low, left, right, ref_left, ref_right, top_left, top_right, low_left, low_right
    )
    fill_windows(ref_ref, sec_ref, halos, ref_win, sec_win)
    tables = (four_ref, spec_ref, lift_ref, corr_ref, lag_ref, wide_ref)
    estimate(
        off_ref, tables, base_ref, ref_win, sec_win, plain_ref, lagged_ref, est_ref, mine
    )
    everyone[me] = mine[...]

    def tell(a, r):
        pltpu.make_async_remote_copy(
            src_ref=mine,
            dst_ref=everyone.at[me],
            send_sem=est_send,
            recv_sem=est_recv,
            device_id=(a, r),
            device_id_type=mesh_ids,
        ).start()

    for_others(tell)
    for group in groups_out[later:]:
        bulk(*group)

    owned = out_ref.shape[1]
    per_plane = cols // LANES
    wide[0, :, :MARGIN] = jnp.zeros((2 * owned, MARGIN), jnp.bfloat16)
    wide[rg_count - 1, :, MARGIN + cols :] = jnp.zeros((2 * owned, MARGIN), jnp.bfloat16)
    told = everyone.at[pl.ds(0, owners - 1)]
    pltpu.make_async_copy(told, told, est_recv).wait()

    lane = lax.broadcasted_iota(jnp.int32, (owned, LANES), 1) // SPACING
    tile = tile_ref[...]

    def turns(plane):
        angle = jnp.zeros((owned, LANES), jnp.float32)
        for a in range(az_count):
            angle = jnp.where(tile == a, everyone[a * rg_count + plane], angle)
        angle = PHASE_RATE * angle
        return jnp.cos(angle), jnp.sin(angle)

    def finish(plane, k, cosine, sine):
        b = plane * per_plane + k
        cols_at = pl.ds(pl.multiple_of(b * LANES, LANES), LANES)
        window = wide[plane, :, pl.ds(pl.multiple_of(k * LANES, LANES), 2 * LANES)]
        s = dot(window, bands[b])
        chip = lane + k * (LANES // SPACING)
        cos_k = jnp.take_along_axis(cosine, chip, axis=1)
        sin_k = jnp.take_along_axis(sine, chip, axis=1)
        s_re = s[:owned]
        s_im = s[owned:]
        out_ref[0, :, cols_at] = (s_re * cos_k + s_im * sin_k).astype(jnp.bfloat16)
        out_ref[1, :, cols_at] = (s_im * cos_k - s_re * sin_k).astype(jnp.bfloat16)

    for d in far_first:
        plane = (rg + rg_count - d) % rg_count
        landed = arrived.at[plane]
        if d == 0:
            landed = landed.at[pl.ds(0, az_count - 1)]
        pltpu.make_async_copy(landed, landed, bulk_recv.at[d]).wait()
        held = arrived[plane].reshape(az_count * ROWS, part)
        for g in range(groups):
            at = MARGIN + g * part
            wide[plane, :, at : at + part] = dot(recv_pick[g], held).astype(jnp.bfloat16)

        @pl.when(plane > 0)
        def _():
            wide[plane - 1, :, MARGIN + cols :] = wide[plane, :, MARGIN : 2 * MARGIN]

        @pl.when(plane < rg_count - 1)
        def _():
            wide[plane + 1, :, :MARGIN] = wide[plane, :, cols : MARGIN + cols]

        cosine, sine = turns(plane)
        inner = per_plane - 2
        unroll = next(u for u in (11, 10, 8, 7, 6, 5, 4, 3, 2, 1) if inner % u == 0)

        def some(i, carry):
            for j in range(unroll):
                finish(plane, 1 + i * unroll + j, cosine, sine)
            return carry

        lax.fori_loop(0, inner // unroll, some, 0)

    def edges(plane, carry):
        cosine, sine = turns(plane)
        finish(plane, 0, cosine, sine)
        finish(plane, per_plane - 1, cosine, sine)
        return carry

    lax.fori_loop(0, rg_count, edges, 0)

    for which, (step_a, step_r, _, _) in enumerate(moves):
        @pl.when(inside(az + step_a, rg + step_r))
        def _():
            halo(which).wait_send()

    gone = outgoing.at[pl.ds(0, owners - 1)]
    pltpu.make_async_copy(gone, gone, bulk_send).wait()
    pltpu.make_async_copy(told, told, est_send).wait()


def fused(offsets, ref, sec, src_row, line_owner, band_start, taps, tables, az_count, rg_count):
    four, spec, lift, corr, lags = tables
    lines = sec.shape[1]
    cols = sec.shape[2]
    chips = cols // SPACING
    blocks = cols // LANES
    owners = az_count * rg_count
    pair_cap = max(2, (lines + 2 * MAX_SHIFT + owners - 1) // owners)
    owner_cap = pair_cap * az_count
    groups = ROWS // (2 * pair_cap)
    part = cols // groups
    far_first = sorted(range(1, rg_count), key=lambda d: abs(d - rg_count // 2)) + [0]
    vmem = pl.BlockSpec(memory_space=pltpu.VMEM)
    lag_wide = np.tile(np.pad(lags, (0, CHIP_LEN - LAG_COUNT)), 2)[None, :]
    bf16 = jnp.bfloat16
    f32 = jnp.float32
    args = (
        offsets, src_row, line_owner, sec, ref, band_start[None], taps, four, spec, lift, corr,
        jnp.asarray(lags)[:, None], jnp.asarray(lag_wide), offsets,
    )
    hbm = pl.BlockSpec(memory_space=pltpu.HBM)
    return pl.pallas_call(
        functools.partial(fused_kernel, pair_cap, tuple(far_first)),
        in_specs=[pl.BlockSpec(memory_space=pltpu.SMEM)] + [hbm] * (len(args) - 1),
        out_specs=(vmem, vmem),
        out_shape=(
            jax.ShapeDtypeStruct((2, 1, chips), f32),
            jax.ShapeDtypeStruct((2, owner_cap, cols * rg_count), bf16),
        ),
        scratch_shapes=[pltpu.VMEM(arg.shape, arg.dtype) for arg in args[1:]] + [
            pltpu.VMEM((groups, 2 * owner_cap, az_count * ROWS), bf16),
            pltpu.VMEM((owner_cap, LANES), f32),
            pltpu.VMEM((owners, ROWS, part), bf16),
            pltpu.VMEM((rg_count, az_count, ROWS, part), bf16),
            pltpu.VMEM((2, MARGIN, cols), bf16),
            pltpu.VMEM((2, MARGIN, cols), bf16),
            pltpu.VMEM((2, lines, LANES), bf16),
            pltpu.VMEM((2, lines, LANES), bf16),
            pltpu.VMEM((2, CHIP_LEN, LANES), bf16),
            pltpu.VMEM((2, CHIP_LEN, LANES), bf16),
            pltpu.VMEM((2, MARGIN, LANES), bf16),
            pltpu.VMEM((2, MARGIN, LANES), bf16),
            pltpu.VMEM((2, MARGIN, LANES), bf16),
            pltpu.VMEM((2, MARGIN, LANES), bf16),
            pltpu.VMEM((2, blocks + 3, CHIP_LEN, LANES), f32),
            pltpu.VMEM((2, blocks + 3, lines + 2 * MARGIN, LANES), f32),
            pltpu.VMEM((chips // 2, LANES), f32),
            pltpu.VMEM((chips // 2, LANES), f32),
            pltpu.VMEM((cols * rg_count // LANES, 2 * LANES, LANES), bf16),
            pltpu.VMEM((rg_count, 2 * owner_cap, cols + 2 * MARGIN), bf16),
            pltpu.VMEM((1, LANES), f32),
            pltpu.VMEM((owners, 1, LANES), f32),
            pltpu.SemaphoreType.DMA((len(args) - 1,)),
            pltpu.SemaphoreType.DMA((10,)),
            pltpu.SemaphoreType.DMA((10,)),
            pltpu.SemaphoreType.DMA,
            pltpu.SemaphoreType.DMA((rg_count,)),
            pltpu.SemaphoreType.DMA,
            pltpu.SemaphoreType.DMA,
        ],
        compiler_params=pltpu.CompilerParams(
            vmem_limit_bytes=VMEM_LIMIT, collective_id=0, has_side_effects=True
        ),
        name="fused",
    )(*args)


def per_device(
    reference_slc, secondary_slc, chip_offsets, src_row, line_owner, band_start, band_taps
):
    shift, lines_out = fused(
        chip_offsets, reference_slc, secondary_slc, src_row, line_owner, band_start, band_taps,
        make_tables(), lax.axis_size("az"), lax.axis_size("rg"),
    )
    return (chip_offsets.astype(jnp.float32) + shift, lines_out)


def solution(mesh):
    return jax.shard_map(
        per_device,
        mesh=mesh,
        in_specs=(
            P(None, "az", "rg"),
            P(None, "az", "rg"),
            P(None, "az", "rg"),
            P(),
            P(),
            P(),
            P(),
        ),
        out_specs=(P(None, "az", "rg"), P(None, ("az", "rg"), None)),
        check_vma=False,
    )
```
